32 devices in a mesh: groups: 2 (over x), seq: 16 (over z, y, core).
Axes of the slice: x: 2, y: 2, z: 4, core: 2. Of those that a mesh axis runs over, the one named last changes fastest.
Arguments:
- features: bfloat16 [16384, 1024], P(('groups', 'seq')), parts along dimension 0, may hold values from -6 to 6
- attention_gain: float32 [1024], replicated, may hold values from 0.1 to 1.9
- qkv_weight: bfloat16 [1024, 3072], replicated, may hold values from -0.1875 to 0.1875
- out_weight: bfloat16 [1024, 1024], replicated, may hold values from -0.1875 to 0.1875
- mlp_gain: float32 [1024], replicated, may hold values from 0.1 to 1.9
- up_weight: bfloat16 [1024, 2048], P(None, 'seq'), may hold values from -0.1875 to 0.1875
- down_weight: bfloat16 [2048, 1024], P('seq'), may hold values from -0.125 to 0.125
- block_columns: int32 [128, 8], P('groups'), parts along dimension 0, may hold values from 0 to 63, as said below
- block_counts: int32 [128], P('groups'), parts along dimension 0, may hold values from 1 to 8, as said below
- global_nodes: int32 [1024], P('groups'), parts along dimension 0, may hold values from 0 to 8191, as said below
Outputs:
- layer_out: bfloat16 [16384, 1024], P(('groups', 'seq')), parts along dimension 0
The draws below stay inside these ranges and needn't reach their ends.
There are 2 independent parts, one for each index of `groups`. The reference program is written for one: setup_inputs(seed, part) draws one part's arguments, and reference() takes and returns one part's arrays. A program takes and returns all parts, laid end to end along the dimension named above; an argument that names none is the same for every part. Nothing has to cross between parts.
Inputs may be any that keep to these rules, and one draw needn't show every extreme that they name: In every row of block_columns the 8 entries are distinct block numbers. `block_counts`: some row block uses all 8 listed column blocks. `global_nodes`: the 512 global nodes are distinct.
All inputs are finite; a program needn't handle non-finite values.
Results may differ from the reference program's by a relative error of at most 0.005.
Values may be sent and summed in bfloat16 or wider, within the bound.
A program may use at most 128 MiB of HBM per device.

```python
import jax
import jax.numpy as jnp
from jax import lax

HEADS = 16
HEAD_DIM = 64
D = 1024
FF = 2048
BLOCK = 128
KMAX = 8
NG = 512
NODES = 8192
NBLK = 64


def draw_block_columns(key, part):
    row_keys = jax.random.split(key, NBLK)
    orders = jax.vmap(lambda row_key: jax.random.permutation(row_key, NBLK))(row_keys)
    offsets = orders[:, :KMAX].astype(jnp.int32)
    rows_ids = jnp.arange(NBLK, dtype=jnp.int32)[:, None]
    return ((rows_ids + offsets) % NBLK).astype(jnp.int32)


def draw_block_counts(key, part):
    counts = jax.random.randint(key, (NBLK,), 1, KMAX + 1, dtype=jnp.int32)
    chosen = jax.random.randint(jax.random.fold_in(key, 7), (), 0, NBLK, dtype=jnp.int32)
    return counts.at[chosen].set(KMAX).astype(jnp.int32)


def draw_global_nodes(key, part):
    return jax.random.permutation(key, NODES)[:NG].astype(jnp.int32)


def level_of(stream_key, shape, cuts, smallest, high):
    loudness, own = 1.0, jax.random.fold_in(stream_key, 6)
    for axis_at, blocks in cuts:
        draws = jnp.exp(jax.random.uniform(jax.random.fold_in(own, axis_at), (blocks,), jnp.float32, smallest / len(cuts), high / len(cuts)))
        loudness = loudness * jnp.repeat(draws, shape[axis_at] // blocks).reshape([-1 if axis == axis_at else 1 for axis in range(len(shape))])
    return loudness


def gaussian(stream_key, extent, width, reach, cuts=(), kind=jnp.bfloat16):
    level = level_of(stream_key, extent, cuts, -0.22, 0.18) if cuts else 1.0
    entries = jax.random.normal(stream_key, extent, jnp.float32) * width * level
    return jnp.minimum(jnp.maximum(entries, -reach), reach).astype(kind)


def setup_inputs(seed: int = 0, part: int = 0) -> dict:
    key_list = jax.random.split(jax.random.key(seed), 11)
    part_splits = jax.random.split(jax.random.fold_in(key_list[10], part), 11)
    features = gaussian(part_splits[0], (NODES, D), 1.0, 6.0, ((0, 16),))
    attention_gain = jnp.clip(1.0 + 0.18 * jax.random.normal(key_list[1], (D,), jnp.float32), 0.1, 1.9)
    qkv_weight = gaussian(key_list[2], (D, 3 * D), D ** -0.5, 0.1875)
    out_weight = gaussian(key_list[3], (D, D), D ** -0.5, 0.1875)
    mlp_gain = jnp.clip(1.0 + 0.18 * jax.random.normal(key_list[4], (D,), jnp.float32), 0.1, 1.9)
    up_weight = gaussian(key_list[5], (D, FF), D ** -0.5, 0.1875, ((1, 16),))
    down_weight = gaussian(key_list[6], (FF, D), FF ** -0.5, 0.125, ((0, 16),))
    block_columns = draw_block_columns(jax.random.fold_in(jax.random.fold_in(key_list[10], part), 71), part)
    block_counts = draw_block_counts(jax.random.fold_in(jax.random.fold_in(key_list[10], part), 71), part)
    global_nodes = draw_global_nodes(jax.random.fold_in(jax.random.fold_in(key_list[10], part), 71), part)
    return {"features": features, "attention_gain": attention_gain, "qkv_weight": qkv_weight, "out_weight": out_weight, "mlp_gain": mlp_gain, "up_weight": up_weight, "down_weight": down_weight, "block_columns": block_columns, "block_counts": block_counts, "global_nodes": global_nodes}


EPS = 1e-05

def layer_norm(values, gain):
    values = values.astype(jnp.float32)
    average = lax.optimization_barrier(jnp.mean(values, axis=-1, keepdims=True))
    centered = values - average
    variance = lax.optimization_barrier(jnp.mean(centered * centered, axis=-1, keepdims=True))
    return centered * lax.rsqrt(variance + EPS) * gain.astype(jnp.float32)

def attend_group(queries, memory_blocks, memory_global, global_block, columns, counts):
    groups, block_rows, head_dim = queries.shape
    slot_count = columns.shape[1]
    in_list = jnp.arange(slot_count, dtype=jnp.int32)[None, :] < counts[:, None]
    picked = memory_blocks[columns].reshape(groups, slot_count * block_rows, 2 * head_dim)
    key_local = picked[:, :, :head_dim].astype(jnp.float32)
    value_local = picked[:, :, head_dim:].astype(jnp.float32)
    query_float = queries.astype(jnp.float32)
    score_scale = head_dim ** (-0.5)
    local_scores = jnp.einsum('gqd,gkd->gqk', query_float, key_local) * score_scale
    key_mask = jnp.repeat(in_list, block_rows, axis=1)[:, None, :]
    local_weights = jnp.where(key_mask, jnp.exp(local_scores), 0.0)
    duplicate = jnp.any(in_list[:, :, None] & (columns[:, :, None] == global_block[None, None, :]), axis=1)
    global_scores = jnp.einsum('gqd,nd->gqn', query_float, memory_global[:, :head_dim].astype(jnp.float32)) * score_scale
    global_weights = jnp.where(duplicate[:, None, :], 0.0, jnp.exp(global_scores))
    totals = lax.optimization_barrier(jnp.sum(local_weights, axis=-1, keepdims=True)) + lax.optimization_barrier(jnp.sum(global_weights, axis=-1, keepdims=True))
    local_probs = (local_weights / totals).astype(jnp.bfloat16)
    global_probs = (global_weights / totals).astype(jnp.bfloat16)
    result = jnp.einsum('gqk,gkd->gqd', local_probs.astype(jnp.float32), value_local)
    result = result + jnp.einsum('gqn,nd->gqd', global_probs.astype(jnp.float32), memory_global[:, head_dim:].astype(jnp.float32))
    return result.astype(jnp.bfloat16)

def reference(features, attention_gain, qkv_weight, out_weight, mlp_gain, up_weight, down_weight, block_columns, block_counts, global_nodes):
    normed = layer_norm(features, attention_gain).astype(jnp.bfloat16)
    packed = jnp.dot(normed, qkv_weight, preferred_element_type=jnp.float32).astype(jnp.bfloat16)
    queries = packed[:, :D].reshape(NODES, HEADS, HEAD_DIM).transpose(1, 0, 2)
    keys_all = packed[:, D:2 * D].reshape(NODES, HEADS, HEAD_DIM)
    values_all = packed[:, 2 * D:].reshape(NODES, HEADS, HEAD_DIM)
    memory_heads = jnp.concatenate((keys_all, values_all), axis=2).transpose(1, 0, 2)
    global_block = (global_nodes // BLOCK).astype(jnp.int32)
    turns = NBLK // 4
    column_groups = block_columns.reshape(turns, 4, KMAX)
    count_groups = block_counts.reshape(turns, 4)

    def one_head(head_pair):
        query_head, memory_head = head_pair
        memory_blocks = memory_head.reshape(NBLK, BLOCK, 2 * HEAD_DIM)
        memory_global = memory_head[global_nodes]
        query_groups = query_head.reshape(turns, 4, BLOCK, HEAD_DIM)

        def one_group(group_item):
            return attend_group(group_item[0], memory_blocks, memory_global, global_block, group_item[1], group_item[2])
        return lax.map(one_group, (query_groups, column_groups, count_groups)).reshape(NODES, HEAD_DIM)
    attended = lax.map(one_head, (queries, memory_heads))
    attended = attended.transpose(1, 0, 2).reshape(NODES, D)
    mixed_rows = features.astype(jnp.float32) + jnp.dot(attended, out_weight, preferred_element_type=jnp.float32)
    normed_mlp = layer_norm(mixed_rows, mlp_gain).astype(jnp.bfloat16)
    hidden = jax.nn.gelu(jnp.dot(normed_mlp, up_weight, preferred_element_type=jnp.float32), approximate=True).astype(jnp.bfloat16)
    return (mixed_rows + jnp.dot(hidden, down_weight, preferred_element_type=jnp.float32)).astype(jnp.bfloat16)
```

```python
import functools

import jax
import jax.numpy as jnp
from jax import lax
from jax.experimental import pallas as pl
from jax.experimental.pallas import tpu as pltpu
from jax.sharding import PartitionSpec as P

HEADS = 16
BLOCK = 128
EPS = 1e-05
MASKED = -1e30


def layer_norm(values, gain):
    values = values.astype(jnp.float32)
    average = jnp.mean(values, axis=-1, keepdims=True)
    centered = values - average
    variance = jnp.mean(centered * centered, axis=-1, keepdims=True)
    return centered * lax.rsqrt(variance + EPS) * gain


def swap_halves(left, right):
    low = lax.broadcasted_iota(jnp.int32, left.shape, 1) < 64
    return (
        jnp.where(low, left, pltpu.roll(right, 64, 1)),
        jnp.where(low, pltpu.roll(left, 64, 1), right),
    )


def attention_kernel(
    n,
    repeat,
    x_ref,
    gain_ref,
    w_ref,
    used_ref,
    spots_ref,
    gidx_ref,
    cols_ref,
    out_ref,
    normed,
    kv_out,
    memory,
    q_out,
    q_in,
    o_out,
    o_in,
    global_sum,
    global_kv,
    bias,
    kv_send,
    kv_recv,
    q_send,
    q_recv,
    o_send,
    o_recv,
):
    rows, width = x_ref.shape
    sub_rows = rows // repeat
    half = sub_rows // 2
    blocks = rows // BLOCK
    slots = cols_ref.shape[1]
    me = lax.axis_index("seq")
    my_head, my_sub = me // repeat, me % repeat
    f32, bf16 = jnp.float32, jnp.bfloat16

    barrier = pltpu.get_barrier_semaphore()

    def greet(step, carry):
        peer = (me + step) % n
        pl.semaphore_signal(
            barrier, inc=1, device_id={"seq": peer}, device_id_type=pl.DeviceIdType.MESH
        )
        return carry

    lax.fori_loop(1, n, greet, 0)

    def kv_copy(head, owner, source):
        return pltpu.make_async_remote_copy(
            src_ref=kv_out.at[head],
            dst_ref=memory.at[pl.ds(source * blocks, blocks)],
            send_sem=kv_send.at[owner],
            recv_sem=kv_recv.at[source],
            device_id={"seq": owner},
            device_id_type=pl.DeviceIdType.MESH,
        )

    def q_copy(owner, source):
        return pltpu.make_async_remote_copy(
            src_ref=q_out.at[owner],
            dst_ref=q_in.at[source],
            send_sem=q_send.at[owner],
            recv_sem=q_recv.at[source],
            device_id={"seq": owner},
            device_id_type=pl.DeviceIdType.MESH,
        )

    def o_copy(home, worker):
        return pltpu.make_async_remote_copy(
            src_ref=o_out.at[home],
            dst_ref=o_in.at[worker],
            send_sem=o_send.at[home],
            recv_sem=o_recv.at[worker],
            device_id={"seq": home},
            device_id_type=pl.DeviceIdType.MESH,
        )

    def norm_rows(i, carry):
        at = pl.ds(pl.multiple_of(i * BLOCK, BLOCK), BLOCK)
        normed[at, :] = layer_norm(x_ref[at, :], gain_ref[...]).astype(bf16)
        return carry

    lax.fori_loop(0, rows // BLOCK, norm_rows, 0)
    pl.semaphore_wait(barrier, n - 1)

    def quad_of(i):
        return (me // (4 * repeat) + 1 + i) % (HEADS // 4)

    def project(first, quad):
        columns = pl.ds(pl.multiple_of(first * width + quad * 256, 256), 256)
        return jnp.dot(normed[...], w_ref[:, columns], preferred_element_type=f32)

    def kv_quad(i, carry):
        quad = quad_of(i)
        keys = project(1, quad)
        values = project(2, quad)
        for pair in range(2):
            at = slice(pair * 128, pair * 128 + 128)
            first, second = swap_halves(keys[:, at], values[:, at])
            kv_out[quad * 4 + 2 * pair] = first.astype(bf16).reshape(blocks, BLOCK, 128)
            kv_out[quad * 4 + 2 * pair + 1] = second.astype(bf16).reshape(blocks, BLOCK, 128)
        for inner in range(4):
            head = quad * 4 + inner
            for sub in range(repeat):
                owner = head * repeat + sub

                @pl.when(owner != me)
                def _():
                    kv_copy(head, owner, me).start()

        return carry

    lax.fori_loop(0, HEADS // 4, kv_quad, 0)

    def q_quad(i, carry):
        quad = quad_of(i)
        queries = project(0, quad) * 0.125
        for pair in range(2):
            both = queries[:, pair * 128 : pair * 128 + 128]
            for sub in range(repeat):
                top = both[sub * sub_rows : sub * sub_rows + half]
                bottom = both[sub * sub_rows + half : (sub + 1) * sub_rows]
                first, second = swap_halves(top, bottom)
                head = quad * 4 + 2 * pair
                q_out[head * repeat + sub] = first.astype(bf16)
                q_out[(head + 1) * repeat + sub] = second.astype(bf16)
        for inner in range(4):
            for sub in range(repeat):
                owner = (quad * 4 + inner) * repeat + sub

                @pl.when(owner != me)
                def _():
                    q_copy(owner, me).start()

        return carry

    lax.fori_loop(0, HEADS // 4, q_quad, 0)

    memory[pl.ds(me * blocks, blocks)] = kv_out[my_head]
    q_in[me] = q_out[me]

    used = used_ref[...]
    global_block = lax.shift_right_logical(spots_ref[...], BLOCK.bit_length() - 1)
    excluded = jnp.zeros((used.shape[0], global_block.shape[1]), f32)
    for j in range(slots):
        listed = used[:, j : j + 1]
        excluded = jnp.where(listed == global_block, MASKED, excluded)
        bias[:, j * BLOCK : (j + 1) * BLOCK] = jnp.broadcast_to(
            jnp.where(listed >= 0, 0.0, MASKED), (used.shape[0], BLOCK)
        )
    bias[:, slots * BLOCK :] = excluded

    global_sum[...] = jnp.zeros_like(global_sum)

    def arrive(step, carry):
        source = (me + n - step) % n

        @pl.when(source != me)
        def _():
            kv_copy(my_head, me, source).wait_recv()

        offset = gidx_ref[...] - source * rows
        spot = lax.broadcasted_iota(jnp.int32, (offset.shape[0], rows), 1)
        chosen = jnp.where(spot == offset, 1.0, 0.0).astype(bf16)
        chunk = memory[pl.ds(source * blocks, blocks)].reshape(rows, 128)
        global_sum[...] += jnp.dot(chosen, chunk, preferred_element_type=f32)
        return carry

    lax.fori_loop(0, n, arrive, 0)
    global_kv[...] = global_sum[...].astype(bf16)

    def serve(step, carry):
        source = (me + n - step) % n

        @pl.when(source != me)
        def _():
            q_copy(me, source).wait_recv()

        packed = q_in[source].astype(f32)
        low = lax.broadcasted_iota(jnp.int32, packed.shape, 1) < 64
        top = jnp.where(low, packed, 0.0).astype(bf16)
        bottom = jnp.where(low, pltpu.roll(packed, 64, 1), 0.0).astype(bf16)
        queries = jnp.concatenate((top, bottom), axis=0)
        results = []
        for r in range(sub_rows // BLOCK):
            block = source * (rows // BLOCK) + my_sub * (sub_rows // BLOCK) + r
            picked = [memory[cols_ref[block, j]] for j in range(slots)]
            kv = jnp.concatenate(picked + [global_kv[...]], axis=0)
            scores = lax.dot_general(
                queries[r * BLOCK : (r + 1) * BLOCK],
                kv,
                (((1,), (1,)), ((), ())),
                preferred_element_type=f32,
            )
            weights = jnp.exp(scores + bias[pl.ds(block, 1), :])
            totals = jnp.sum(weights, axis=1, keepdims=True)
            scale = jnp.where(totals > 1.0, 2.0**-10, 1.0)
            probs = (weights * (1.0 / (totals * scale))).astype(bf16)
            results.append(jnp.dot(probs, kv, preferred_element_type=f32) * scale)
        result = jnp.concatenate(results, axis=0)
        top, bottom = result[:half], result[half:]
        o_out[source] = jnp.where(low, pltpu.roll(top, 64, 1), bottom).astype(bf16)

        @pl.when(source != me)
        def _():
            o_copy(source, me).start()

        return carry

    lax.fori_loop(0, n, serve, 0)
    o_in[me] = o_out[me]

    def settle(step, carry):
        peer = (me + step) % n
        o_copy(me, peer).wait_recv()
        kv_copy(peer // repeat, peer, me).wait_send()
        q_copy(peer, me).wait_send()
        o_copy(peer, me).wait_send()
        return carry

    lax.fori_loop(1, n, settle, 0)

    for pair in range(HEADS // 2):
        for sub in range(repeat):
            first = o_in[2 * pair * repeat + sub].astype(f32)
            second = o_in[(2 * pair + 1) * repeat + sub].astype(f32)
            top, bottom = swap_halves(first, second)
            at = slice(pair * 128, pair * 128 + 128)
            out_ref[sub * sub_rows : sub * sub_rows + half, at] = top.astype(bf16)
            out_ref[sub * sub_rows + half : (sub + 1) * sub_rows, at] = bottom.astype(bf16)


def attend(features, gain, weight, used, global_nodes, columns):
    n = lax.axis_size("seq")
    repeat = n // HEADS
    rows, width = features.shape
    half = rows // repeat // 2
    globals_count = global_nodes.shape[0]
    keys = columns.shape[1] * BLOCK + globals_count
    bf16 = jnp.bfloat16
    vmem = pl.BlockSpec(memory_space=pltpu.VMEM)
    flops = 2 * rows * width * 3 * width + 4 * rows * HEADS * 64 * keys
    return pl.pallas_call(
        functools.partial(attention_kernel, n, repeat),
        out_shape=jax.ShapeDtypeStruct((rows, width), bf16),
        in_specs=[vmem] * 6 + [pl.BlockSpec(memory_space=pltpu.SMEM)],
        out_specs=vmem,
        scratch_shapes=[
            pltpu.VMEM((rows, width), bf16),
            pltpu.VMEM((HEADS, rows // BLOCK, BLOCK, 128), bf16),
            pltpu.VMEM((n * rows // BLOCK, BLOCK, 128), bf16),
            pltpu.VMEM((n, half, 128), bf16),
            pltpu.VMEM((n, half, 128), bf16),
            pltpu.VMEM((n, half, 128), bf16),
            pltpu.VMEM((n, half, 128), bf16),
            pltpu.VMEM((globals_count, 128), jnp.float32),
            pltpu.VMEM((globals_count, 128), bf16),
            pltpu.VMEM((columns.shape[0], keys), jnp.float32),
        ]
        + [pltpu.SemaphoreType.DMA((n,))] * 6,
        compiler_params=pltpu.CompilerParams(
            collective_id=0, has_side_effects=True, vmem_limit_bytes=48 * 2**20
        ),
        cost_estimate=pl.CostEstimate(
            flops=flops * 16, bytes_accessed=2**24, transcendentals=rows * HEADS * keys
        ),
        name="attend",
    )(features, gain[None, :], weight, used, global_nodes[None, :], global_nodes[:, None], columns)


def on_device(
    features,
    attention_gain,
    qkv_weight,
    out_weight,
    mlp_gain,
    up_weight,
    down_weight,
    block_columns,
    block_counts,
    global_nodes,
):
    slots = block_columns.shape[1]
    in_list = jnp.arange(slots, dtype=jnp.int32)[None, :] < block_counts[:, None]
    used = jnp.where(in_list, block_columns, -1)
    groups = lax.axis_size("groups")
    part = up_weight.shape[1] // groups
    first = lax.axis_index("groups") * part
    shard = jnp.concatenate(
        (
            lax.dynamic_slice_in_dim(up_weight.T, first, part, 0)[None],
            lax.dynamic_slice_in_dim(down_weight, first, part, 0)[None],
        ),
        axis=0,
    )
    gathered = lax.all_gather(shard, ("seq", "groups"), axis=1, tiled=True)
    up_rows, down_rows = gathered[0], gathered[1]
    attended_rows = attend(
        features, attention_gain, qkv_weight, used, global_nodes, block_columns
    )
    mixed_rows = features.astype(jnp.float32) + jnp.dot(
        attended_rows, out_weight, preferred_element_type=jnp.float32
    )
    normed_mlp = layer_norm(mixed_rows, mlp_gain).astype(jnp.bfloat16)
    hidden = jax.nn.gelu(
        lax.dot_general(
            normed_mlp,
            up_rows,
            (((1,), (1,)), ((), ())),
            preferred_element_type=jnp.float32,
        ),
        approximate=True,
    ).astype(jnp.bfloat16)
    reduced = jnp.dot(
        hidden,
        down_rows,
        preferred_element_type=jnp.float32,
    )
    return (mixed_rows + reduced).astype(jnp.bfloat16)


def layer_kernel(
    x_ref,
    gain_ref,
    mlp_gain_ref,
    spots_ref,
    cols_ref,
    counts_ref,
    w_hbm,
    mix_hbm,
    up_hbm,
    down_hbm,
    out_ref,
    w_ref,
    mix_ref,
    up_all,
    down_all,
    normed,
    kv_out,
    memory,
    q_out,
    q_in,
    o_out,
    o_in,
    global_sum,
    global_kv,
    mixed,
    hidden,
    load_sem,
    kv_send,
    kv_recv,
    q_send,
    q_recv,
    o_send,
    o_recv,
    z_send,
    z_recv,
    swap_send,
    swap_recv,
):
    n = HEADS
    rows, width = x_ref.shape
    half = rows // 2
    blocks = rows // BLOCK
    slots = cols_ref.shape[0]
    count = spots_ref.shape[1]
    deep = n // 4
    me, g = lax.axis_index("seq"), lax.axis_index("groups")
    z, y, c = me // 4, me // 2 % 2, me % 2
    f32, bf16 = jnp.float32, jnp.bfloat16

    part = (up_hbm.shape[0] // 2, down_hbm.shape[0] // 2)

    def hop_views(piece):
        return [
            whole.at[piece, y, c, pl.ds(g * size, size)]
            for whole, size in zip((up_all, down_all), part)
        ]

    def load(source, target, at):
        return pltpu.make_async_copy(source, target, load_sem.at[at])

    loads = [
        load(up_hbm.at[pl.ds(g * part[0], part[0])], hop_views(z)[0], 0),
        load(down_hbm.at[pl.ds(g * part[1], part[1])], hop_views(z)[1], 1),
        load(w_hbm.at[:, pl.ds(width, 2 * width)], w_ref.at[:, pl.ds(width, 2 * width)], 2),
        load(w_hbm.at[:, pl.ds(0, width)], w_ref.at[:, pl.ds(0, width)], 3),
        load(mix_hbm, mix_ref, 4),
    ]
    for item in loads:
        item.start()

    barrier = pltpu.get_barrier_semaphore()

    def greet(step, carry):
        pl.semaphore_signal(
            barrier,
            inc=1,
            device_id={"seq": (me + step) % n},
            device_id_type=pl.DeviceIdType.MESH,
        )
        return carry

    lax.fori_loop(1, n, greet, 0)
    pl.semaphore_signal(
        barrier,
        inc=1,
        device_id={"groups": 1 - g, "seq": me},
        device_id_type=pl.DeviceIdType.MESH,
    )

    def remote(source, target, send, recv, where):
        return pltpu.make_async_remote_copy(
            src_ref=source,
            dst_ref=target,
            send_sem=send,
            recv_sem=recv,
            device_id=where,
            device_id_type=pl.DeviceIdType.MESH,
        )

    def kv_copy(owner, source):
        return remote(
            kv_out.at[owner],
            memory.at[pl.ds(source * blocks, blocks)],
            kv_send.at[owner],
            kv_recv.at[source],
            {"seq": owner},
        )

    def q_copy(owner, source):
        return remote(
            q_out.at[owner], q_in.at[source], q_send.at[owner], q_recv.at[source], {"seq": owner}
        )

    def o_copy(home, worker):
        return remote(
            o_out.at[home], o_in.at[worker], o_send.at[home], o_recv.at[worker], {"seq": home}
        )

    def hop_copies(way, hop, piece, to):
        return [
            remote(
                view,
                view,
                z_send.at[way, hop - 1, kind],
                z_recv.at[piece, kind],
                {"seq": to * 4 + y * 2 + c},
            )
            for kind, view in enumerate(hop_views(piece))
        ]

    def hop_sends(hop, act):
        for way, d in enumerate((1, -1)):
            piece, to = z - d * (hop - 1), z + d

            @pl.when((piece >= 0) & (piece < deep) & (to >= 0) & (to < deep))
            def _():
                for copy in hop_copies(way, hop, piece, to):
                    act(copy)

    def hop_waits(hop):
        for way, d in enumerate((1, -1)):
            piece = z - d * hop

            @pl.when((piece >= 0) & (piece < deep))
            def _():
                for copy in hop_copies(way, hop, piece, z):
                    copy.wait_recv()

    def y_copies(row):
        to = {"seq": me + 2 - 4 * y}
        return [
            remote(
                whole.at[:, row, c, pl.ds(g * size, size)],
                whole.at[:, row, c, pl.ds(g * size, size)],
                swap_send.at[0, kind],
                swap_recv.at[0, kind],
                to,
            )
            for kind, (whole, size) in enumerate(zip((up_all, down_all), part))
        ]

    def x_copies(turn, row, side):
        to = {"groups": 1 - g, "seq": me}
        return [
            remote(
                whole.at[:, row, c, pl.ds(side * size, size)],
                whole.at[:, row, c, pl.ds(side * size, size)],
                swap_send.at[1 + turn, kind],
                swap_recv.at[1 + turn, kind],
                to,
            )
            for kind, (whole, size) in enumerate(zip((up_all, down_all), part))
        ]

    def core_copies(core):
        to = {"seq": me + 1 - 2 * c}
        return [
            remote(
                whole.at[:, :, core],
                whole.at[:, :, core],
                swap_send.at[3, kind],
                swap_recv.at[3, kind],
                to,
            )
            for kind, whole in enumerate((up_all, down_all))
        ]

    def start(copies):
        for copy in copies:
            copy.start()

    def arrived(copies):
        for copy in copies:
            copy.wait_recv()

    def norm_rows(i, carry):
        at = pl.ds(pl.multiple_of(i * BLOCK, BLOCK), BLOCK)
        normed[at, :] = layer_norm(x_ref[at, :], gain_ref[...]).astype(bf16)
        return carry

    loads[0].wait()
    loads[1].wait()
    pl.semaphore_wait(barrier, n)
    hop_sends(1, lambda copy: copy.start())
    lax.fori_loop(0, blocks, norm_rows, 0)

    def quad_of(i):
        flip_high, flip_low = i // 2, i % 2
        return (z // 2 + flip_high) % 2 * 2 + (z % 2 + flip_low) % 2

    def member(quad, inner):
        return quad * 4 + (me + inner) % 4

    def project(first, quad):
        columns = pl.ds(pl.multiple_of(first * width + quad * 256, 256), 256)
        return jnp.dot(normed[...], w_ref[:, columns], preferred_element_type=f32)

    loads[2].wait()

    def kv_quad(i, carry):
        quad = quad_of(i)
        keys = project(1, quad)
        values = project(2, quad)
        for pair in range(2):
            at = slice(pair * 128, pair * 128 + 128)
            first, second = swap_halves(keys[:, at], values[:, at])
            kv_out[quad * 4 + 2 * pair] = first.astype(bf16).reshape(blocks, BLOCK, 128)
            kv_out[quad * 4 + 2 * pair + 1] = second.astype(bf16).reshape(blocks, BLOCK, 128)
        return carry

    def q_quad(i, carry):
        quad = quad_of(i)
        queries = project(0, quad) * 0.125
        for pair in range(2):
            both = queries[:, pair * 128 : pair * 128 + 128]
            first, second = swap_halves(both[:half], both[half:])
            head = quad * 4 + 2 * pair
            q_out[head] = first.astype(bf16)
            q_out[head + 1] = second.astype(bf16)
        return carry

    def send_each(first, last, copy):
        def send(i, carry):
            owner = member(quad_of(i // 4), i)

            @pl.when(owner != me)
            def _():
                copy(owner, me).start()

            return carry

        lax.fori_loop(first * 4, last * 4, send, 0)

    def kv_quad_sent(i, carry):
        kv_quad(i, carry)
        send_each(i, i + 1, kv_copy)
        return carry

    lax.fori_loop(0, 2, kv_quad_sent, 0)
    hop_waits(1)
    hop_sends(2, lambda copy: copy.start())
    lax.fori_loop(2, 4, kv_quad, 0)
    loads[3].wait()
    lax.fori_loop(0, 4, q_quad, 0)
    hop_waits(2)
    hop_sends(3, lambda copy: copy.start())
    send_each(2, 4, kv_copy)
    send_each(2, 4, q_copy)
    send_each(0, 2, q_copy)

    memory[pl.ds(me * blocks, blocks)] = kv_out[me]
    q_in[me] = q_out[me]

    global_sum[...] = jnp.zeros_like(global_sum)
    spots = spots_ref[...]
    spots_column = jnp.transpose(jnp.broadcast_to(spots.astype(f32), (128, count)))
    spots_column = spots_column[:, :1].astype(jnp.int32)

    def arrive(step, carry):
        source = member(quad_of(step // 4), step)

        @pl.when(source != me)
        def _():
            kv_copy(me, source).wait_recv()

        offset = spots_column - source * rows
        spot = lax.broadcasted_iota(jnp.int32, (count, rows), 1)
        chosen = jnp.where(spot == offset, 1.0, 0.0).astype(bf16)
        chunk = memory[pl.ds(source * blocks, blocks)].reshape(rows, 128)
        global_sum[...] += jnp.dot(chosen, chunk, preferred_element_type=f32)

        @pl.when(step == 4)
        def _():
            hop_waits(3)
            start(y_copies(y) + x_copies(0, y, g))

        return carry

    lax.fori_loop(0, n, arrive, 0)
    global_kv[...] = global_sum[...].astype(bf16)
    arrived(y_copies(1 - y))
    start(x_copies(1, 1 - y, g))
    spot_block = lax.shift_right_logical(spots, BLOCK.bit_length() - 1)

    def serve(step, carry):
        source = member(quad_of(step // 4), step)

        @pl.when(source != me)
        def _():
            q_copy(me, source).wait_recv()

        packed = q_in[source].astype(f32)
        low = lax.broadcasted_iota(jnp.int32, packed.shape, 1) < 64
        top = jnp.where(low, packed, 0.0).astype(bf16)
        bottom = jnp.where(low, pltpu.roll(packed, 64, 1), 0.0).astype(bf16)
        queries = jnp.concatenate((top, bottom), axis=0)
        results = []
        for r in range(blocks):
            block = source * blocks + r
            used = counts_ref[block]
            excluded = jnp.zeros((1, count), f32)
            parts = []
            for j in range(slots):
                listed = jnp.where(j < used, cols_ref[j, block], -1)
                excluded = jnp.where(spot_block == listed, MASKED, excluded)
                parts.append(jnp.full((1, BLOCK), jnp.where(j < used, 0.0, MASKED), f32))
            bias = jnp.concatenate(parts + [excluded], axis=1)
            picked = [memory[cols_ref[j, block]] for j in range(slots)]
            kv = jnp.concatenate(picked + [global_kv[...]], axis=0)
            scores = lax.dot_general(
                queries[r * BLOCK : (r + 1) * BLOCK],
                kv,
                (((1,), (1,)), ((), ())),
                preferred_element_type=f32,
            )
            weights = jnp.exp(scores + bias)
            totals = jnp.sum(weights, axis=1, keepdims=True)
            scale = jnp.where(totals > 1.0, 2.0**-10, 1.0)
            probs = (weights * (1.0 / (totals * scale))).astype(bf16)
            results.append(jnp.dot(probs, kv, preferred_element_type=f32) * scale)
        result = jnp.concatenate(results, axis=0)
        top, bottom = result[:half], result[half:]
        o_out[source] = jnp.where(low, pltpu.roll(top, 64, 1), bottom).astype(bf16)

        @pl.when(source != me)
        def _():
            o_copy(source, me).start()

        @pl.when(step == n - 4)
        def _():
            arrived(x_copies(0, y, 1 - g) + x_copies(1, 1 - y, 1 - g))
            start(core_copies(c))

        return carry

    lax.fori_loop(0, n, serve, 0)
    o_in[me] = o_out[me]

    def settle(step, carry):
        peer = (me + step) % n
        kv_copy(peer, me).wait_send()
        q_copy(peer, me).wait_send()
        o_copy(me, peer).wait_recv()
        return carry

    lax.fori_loop(1, n, settle, 0)

    for pair in range(n // 2):
        first = o_in[2 * pair].astype(f32)
        second = o_in[2 * pair + 1].astype(f32)
        top, bottom = swap_halves(first, second)
        at = slice(pair * 128, pair * 128 + 128)
        normed[:half, at] = top.astype(bf16)
        normed[half:, at] = bottom.astype(bf16)

    loads[4].wait()

    def mix(i, carry):
        at = pl.ds(pl.multiple_of(i * 256, 256), 256)
        mixed[:, at] = x_ref[:, at].astype(f32) + jnp.dot(
            normed[...], mix_ref[:, at], preferred_element_type=f32
        )
        return carry

    lax.fori_loop(0, width // 256, mix, 0)

    def norm_again(i, carry):
        at = pl.ds(pl.multiple_of(i * BLOCK, BLOCK), BLOCK)
        normed[at, :] = layer_norm(mixed[at, :], mlp_gain_ref[...]).astype(bf16)
        return carry

    lax.fori_loop(0, blocks, norm_again, 0)
    arrived(core_copies(1 - c))

    def expand(i, carry):
        up = jnp.concatenate((up_all[i // 2, i % 2, 0], up_all[i // 2, i % 2, 1]), axis=1)
        units = jnp.dot(normed[...], up, preferred_element_type=f32)
        hidden[:, pl.ds(pl.multiple_of(i * 256, 256), 256)] = jax.nn.gelu(
            units, approximate=True
        ).astype(bf16)
        return carry

    lax.fori_loop(0, n // 2, expand, 0)

    def contract(i, carry):
        at = pl.ds(pl.multiple_of(i * 256, 256), 256)
        down = down_all[:, :, :, :, at].reshape(hidden.shape[1], 256)
        out_ref[:, at] = (
            mixed[:, at] + jnp.dot(hidden[...], down, preferred_element_type=f32)
        ).astype(bf16)
        return carry

    lax.fori_loop(0, width // 256, contract, 0)

    def finish(step, carry):
        o_copy((me + step) % n, me).wait_send()
        return carry

    lax.fori_loop(1, n, finish, 0)
    for hop in range(1, deep):
        hop_sends(hop, lambda copy: copy.wait_send())
    for copy in y_copies(y) + x_copies(0, y, g) + x_copies(1, 1 - y, g) + core_copies(c):
        copy.wait_send()


def whole_layer(
    features,
    attention_gain,
    qkv_weight,
    out_weight,
    mlp_gain,
    up_weight,
    down_weight,
    block_columns,
    block_counts,
    global_nodes,
):
    n = HEADS
    rows, width = features.shape
    half, blocks, deep = rows // 2, rows // BLOCK, n // 4
    count, unit = global_nodes.shape[0], up_weight.shape[1]
    keys = block_columns.shape[1] * BLOCK + count
    f32, bf16 = jnp.float32, jnp.bfloat16
    vmem = pl.BlockSpec(memory_space=pltpu.VMEM)
    smem = pl.BlockSpec(memory_space=pltpu.SMEM)
    hbm = pl.BlockSpec(memory_space=pl.ANY)
    flops = 2 * rows * width * (4 * width + 2 * n * unit) + 4 * rows * HEADS * 64 * keys
    dma = pltpu.SemaphoreType.DMA
    return pl.pallas_call(
        layer_kernel,
        out_shape=jax.ShapeDtypeStruct((rows, width), bf16),
        in_specs=[vmem] * 4 + [smem] * 2 + [hbm] * 4,
        out_specs=vmem,
        scratch_shapes=[
            pltpu.VMEM(qkv_weight.shape, bf16),
            pltpu.VMEM(out_weight.shape, bf16),
            pltpu.VMEM((deep, 2, 2, width, unit), bf16),
            pltpu.VMEM((deep, 2, 2, unit, width), bf16),
            pltpu.VMEM((rows, width), bf16),
            pltpu.VMEM((n, blocks, BLOCK, 128), bf16),
            pltpu.VMEM((n * blocks, BLOCK, 128), bf16),
            pltpu.VMEM((n, half, 128), bf16),
            pltpu.VMEM((n, half, 128), bf16),
            pltpu.VMEM((n, half, 128), bf16),
            pltpu.VMEM((n, half, 128), bf16),
            pltpu.VMEM((count, 128), f32),
            pltpu.VMEM((count, 128), bf16),
            pltpu.VMEM((rows, width), f32),
            pltpu.VMEM((rows, n * unit), bf16),
            dma((5,)),
        ]
        + [dma((n,))] * 6
        + [dma((2, deep - 1, 2)), dma((deep, 2)), dma((4, 2)), dma((4, 2))],
        compiler_params=pltpu.CompilerParams(
            collective_id=1, has_side_effects=True, vmem_limit_bytes=56 * 2**20
        ),
        cost_estimate=pl.CostEstimate(
            flops=flops, bytes_accessed=2**24, transcendentals=rows * HEADS * keys
        ),
        name="layer",
    )(
        features,
        attention_gain[None, :],
        mlp_gain[None, :],
        global_nodes[None, :],
        block_columns.T,
        block_counts,
        qkv_weight,
        out_weight,
        up_weight,
        down_weight,
    )


def solution(mesh):
    in_specs = (
        P(("groups", "seq"), None),
        P(),
        P(),
        P(),
        P(),
        P(None, "seq"),
        P("seq", None),
        P("groups", None),
        P("groups"),
        P("groups"),
    )
    out_specs = P(("groups", "seq"), None)
    step = whole_layer if mesh.shape["seq"] == HEADS and mesh.shape["groups"] == 2 else on_device
    return jax.shard_map(
        step, mesh=mesh, in_specs=in_specs, out_specs=out_specs, check_vma=False
    )
```

```python
import functools

import jax
import jax.numpy as jnp
from jax import lax
from jax.experimental import pallas as pl
from jax.experimental.pallas import tpu as pltpu
from jax.sharding import PartitionSpec as P

HEADS = 16
BLOCK = 128
EPS = 1e-05
MASKED = -1e30


def layer_norm(values, gain):
    values = values.astype(jnp.float32)
    average = jnp.mean(values, axis=-1, keepdims=True)
    centered = values - average
    variance = jnp.mean(centered * centered, axis=-1, keepdims=True)
    return centered * lax.rsqrt(variance + EPS) * gain


def swap_halves(left, right):
    low = lax.broadcasted_iota(jnp.int32, left.shape, 1) < 64
    return (
        jnp.where(low, left, pltpu.roll(right, 64, 1)),
        jnp.where(low, pltpu.roll(left, 64, 1), right),
    )


def attention_kernel(
    n,
    repeat,
    x_ref,
    gain_ref,
    w_ref,
    used_ref,
    spots_ref,
    gidx_ref,
    cols_ref,
    out_ref,
    normed,
    kv_out,
    memory,
    q_out,
    q_in,
    o_out,
    o_in,
    global_sum,
    global_kv,
    bias,
    kv_send,
    kv_recv,
    q_send,
    q_recv,
    o_send,
    o_recv,
):
    rows, width = x_ref.shape
    sub_rows = rows // repeat
    half = sub_rows // 2
    blocks = rows // BLOCK
    slots = cols_ref.shape[1]
    me = lax.axis_index("seq")
    my_head, my_sub = me // repeat, me % repeat
    f32, bf16 = jnp.float32, jnp.bfloat16

    barrier = pltpu.get_barrier_semaphore()

    def greet(step, carry):
        peer = (me + step) % n
        pl.semaphore_signal(
            barrier, inc=1, device_id={"seq": peer}, device_id_type=pl.DeviceIdType.MESH
        )
        return carry

    lax.fori_loop(1, n, greet, 0)

    def kv_copy(head, owner, source):
        return pltpu.make_async_remote_copy(
            src_ref=kv_out.at[head],
            dst_ref=memory.at[pl.ds(source * blocks, blocks)],
            send_sem=kv_send.at[owner],
            recv_sem=kv_recv.at[source],
            device_id={"seq": owner},
            device_id_type=pl.DeviceIdType.MESH,
        )

    def q_copy(owner, source):
        return pltpu.make_async_remote_copy(
            src_ref=q_out.at[owner],
            dst_ref=q_in.at[source],
            send_sem=q_send.at[owner],
            recv_sem=q_recv.at[source],
            device_id={"seq": owner},
            device_id_type=pl.DeviceIdType.MESH,
        )

    def o_copy(home, worker):
        return pltpu.make_async_remote_copy(
            src_ref=o_out.at[home],
            dst_ref=o_in.at[worker],
            send_sem=o_send.at[home],
            recv_sem=o_recv.at[worker],
            device_id={"seq": home},
            device_id_type=pl.DeviceIdType.MESH,
        )

    def norm_rows(i, carry):
        at = pl.ds(pl.multiple_of(i * BLOCK, BLOCK), BLOCK)
        normed[at, :] = layer_norm(x_ref[at, :], gain_ref[...]).astype(bf16)
        return carry

    lax.fori_loop(0, rows // BLOCK, norm_rows, 0)
    pl.semaphore_wait(barrier, n - 1)

    def quad_of(i):
        return (me // (4 * repeat) + 1 + i) % (HEADS // 4)

    def project(first, quad):
        columns = pl.ds(pl.multiple_of(first * width + quad * 256, 256), 256)
        return jnp.dot(normed[...], w_ref[:, columns], preferred_element_type=f32)

    def kv_quad(i, carry):
        quad = quad_of(i)
        keys = project(1, quad)
        values = project(2, quad)
        for pair in range(2):
            at = slice(pair * 128, pair * 128 + 128)
            first, second = swap_halves(keys[:, at], values[:, at])
            kv_out[quad * 4 + 2 * pair] = first.astype(bf16).reshape(blocks, BLOCK, 128)
            kv_out[quad * 4 + 2 * pair + 1] = second.astype(bf16).reshape(blocks, BLOCK, 128)
        for inner in range(4):
            head = quad * 4 + inner
            for sub in range(repeat):
                owner = head * repeat + sub

                @pl.when(owner != me)
                def _():
                    kv_copy(head, owner, me).start()

        return carry

    lax.fori_loop(0, HEADS // 4, kv_quad, 0)

    def q_quad(i, carry):
        quad = quad_of(i)
        queries = project(0, quad) * 0.125
        for pair in range(2):
            both = queries[:, pair * 128 : pair * 128 + 128]
            for sub in range(repeat):
                top = both[sub * sub_rows : sub * sub_rows + half]
                bottom = both[sub * sub_rows + half : (sub + 1) * sub_rows]
                first, second = swap_halves(top, bottom)
                head = quad * 4 + 2 * pair
                q_out[head * repeat + sub] = first.astype(bf16)
                q_out[(head + 1) * repeat + sub] = second.astype(bf16)
        for inner in range(4):
            for sub in range(repeat):
                owner = (quad * 4 + inner) * repeat + sub

                @pl.when(owner != me)
                def _():
                    q_copy(owner, me).start()

        return carry

    lax.fori_loop(0, HEADS // 4, q_quad, 0)

    memory[pl.ds(me * blocks, blocks)] = kv_out[my_head]
    q_in[me] = q_out[me]

    used = used_ref[...]
    global_block = lax.shift_right_logical(spots_ref[...], BLOCK.bit_length() - 1)
    excluded = jnp.zeros((used.shape[0], global_block.shape[1]), f32)
    for j in range(slots):
        listed = used[:, j : j + 1]
        excluded = jnp.where(listed == global_block, MASKED, excluded)
        bias[:, j * BLOCK : (j + 1) * BLOCK] = jnp.broadcast_to(
            jnp.where(listed >= 0, 0.0, MASKED), (used.shape[0], BLOCK)
        )
    bias[:, slots * BLOCK :] = excluded

    global_sum[...] = jnp.zeros_like(global_sum)

    def arrive(step, carry):
        source = (me + n - step) % n

        @pl.when(source != me)
        def _():
            kv_copy(my_head, me, source).wait_recv()

        offset = gidx_ref[...] - source * rows
        spot = lax.broadcasted_iota(jnp.int32, (offset.shape[0], rows), 1)
        chosen = jnp.where(spot == offset, 1.0, 0.0).astype(bf16)
        chunk = memory[pl.ds(source * blocks, blocks)].reshape(rows, 128)
        global_sum[...] += jnp.dot(chosen, chunk, preferred_element_type=f32)
        return carry

    lax.fori_loop(0, n, arrive, 0)
    global_kv[...] = global_sum[...].astype(bf16)

    def serve(step, carry):
        source = (me + n - step) % n

        @pl.when(source != me)
        def _():
            q_copy(me, source).wait_recv()

        packed = q_in[source].astype(f32)
        low = lax.broadcasted_iota(jnp.int32, packed.shape, 1) < 64
        top = jnp.where(low, packed, 0.0).astype(bf16)
        bottom = jnp.where(low, pltpu.roll(packed, 64, 1), 0.0).astype(bf16)
        queries = jnp.concatenate((top, bottom), axis=0)
        results = []
        for r in range(sub_rows // BLOCK):
            block = source * (rows // BLOCK) + my_sub * (sub_rows // BLOCK) + r
            picked = [memory[cols_ref[block, j]] for j in range(slots)]
            kv = jnp.concatenate(picked + [global_kv[...]], axis=0)
            scores = lax.dot_general(
                queries[r * BLOCK : (r + 1) * BLOCK],
                kv,
                (((1,), (1,)), ((), ())),
                preferred_element_type=f32,
            )
            weights = jnp.exp(scores + bias[pl.ds(block, 1), :])
            totals = jnp.sum(weights, axis=1, keepdims=True)
            scale = jnp.where(totals > 1.0, 2.0**-10, 1.0)
            probs = (weights * (1.0 / (totals * scale))).astype(bf16)
            results.append(jnp.dot(probs, kv, preferred_element_type=f32) * scale)
        result = jnp.concatenate(results, axis=0)
        top, bottom = result[:half], result[half:]
        o_out[source] = jnp.where(low, pltpu.roll(top, 64, 1), bottom).astype(bf16)

        @pl.when(source != me)
        def _():
            o_copy(source, me).start()

        return carry

    lax.fori_loop(0, n, serve, 0)
    o_in[me] = o_out[me]

    def settle(step, carry):
        peer = (me + step) % n
        o_copy(me, peer).wait_recv()
        kv_copy(peer // repeat, peer, me).wait_send()
        q_copy(peer, me).wait_send()
        o_copy(peer, me).wait_send()
        return carry

    lax.fori_loop(1, n, settle, 0)

    for pair in range(HEADS // 2):
        for sub in range(repeat):
            first = o_in[2 * pair * repeat + sub].astype(f32)
            second = o_in[(2 * pair + 1) * repeat + sub].astype(f32)
            top, bottom = swap_halves(first, second)
            at = slice(pair * 128, pair * 128 + 128)
            out_ref[sub * sub_rows : sub * sub_rows + half, at] = top.astype(bf16)
            out_ref[sub * sub_rows + half : (sub + 1) * sub_rows, at] = bottom.astype(bf16)


def attend(features, gain, weight, used, global_nodes, columns):
    n = lax.axis_size("seq")
    repeat = n // HEADS
    rows, width = features.shape
    half = rows // repeat // 2
    globals_count = global_nodes.shape[0]
    keys = columns.shape[1] * BLOCK + globals_count
    bf16 = jnp.bfloat16
    vmem = pl.BlockSpec(memory_space=pltpu.VMEM)
    flops = 2 * rows * width * 3 * width + 4 * rows * HEADS * 64 * keys
    return pl.pallas_call(
        functools.partial(attention_kernel, n, repeat),
        out_shape=jax.ShapeDtypeStruct((rows, width), bf16),
        in_specs=[vmem] * 6 + [pl.BlockSpec(memory_space=pltpu.SMEM)],
        out_specs=vmem,
        scratch_shapes=[
            pltpu.VMEM((rows, width), bf16),
            pltpu.VMEM((HEADS, rows // BLOCK, BLOCK, 128), bf16),
            pltpu.VMEM((n * rows // BLOCK, BLOCK, 128), bf16),
            pltpu.VMEM((n, half, 128), bf16),
            pltpu.VMEM((n, half, 128), bf16),
            pltpu.VMEM((n, half, 128), bf16),
            pltpu.VMEM((n, half, 128), bf16),
            pltpu.VMEM((globals_count, 128), jnp.float32),
            pltpu.VMEM((globals_count, 128), bf16),
            pltpu.VMEM((columns.shape[0], keys), jnp.float32),
        ]
        + [pltpu.SemaphoreType.DMA((n,))] * 6,
        compiler_params=pltpu.CompilerParams(
            collective_id=0, has_side_effects=True, vmem_limit_bytes=48 * 2**20
        ),
        cost_estimate=pl.CostEstimate(
            flops=flops * 16, bytes_accessed=2**24, transcendentals=rows * HEADS * keys
        ),
        name="attend",
    )(features, gain[None, :], weight, used, global_nodes[None, :], global_nodes[:, None], columns)


def on_device(
    features,
    attention_gain,
    qkv_weight,
    out_weight,
    mlp_gain,
    up_weight,
    down_weight,
    block_columns,
    block_counts,
    global_nodes,
):
    slots = block_columns.shape[1]
    in_list = jnp.arange(slots, dtype=jnp.int32)[None, :] < block_counts[:, None]
    used = jnp.where(in_list, block_columns, -1)
    groups = lax.axis_size("groups")
    part = up_weight.shape[1] // groups
    first = lax.axis_index("groups") * part
    shard = jnp.concatenate(
        (
            lax.dynamic_slice_in_dim(up_weight.T, first, part, 0)[None],
            lax.dynamic_slice_in_dim(down_weight, first, part, 0)[None],
        ),
        axis=0,
    )
    gathered = lax.all_gather(shard, ("seq", "groups"), axis=1, tiled=True)
    up_rows, down_rows = gathered[0], gathered[1]
    attended_rows = attend(
        features, attention_gain, qkv_weight, used, global_nodes, block_columns
    )
    mixed_rows = features.astype(jnp.float32) + jnp.dot(
        attended_rows, out_weight, preferred_element_type=jnp.float32
    )
    normed_mlp = layer_norm(mixed_rows, mlp_gain).astype(jnp.bfloat16)
    hidden = jax.nn.gelu(
        lax.dot_general(
            normed_mlp,
            up_rows,
            (((1,), (1,)), ((), ())),
            preferred_element_type=jnp.float32,
        ),
        approximate=True,
    ).astype(jnp.bfloat16)
    reduced = jnp.dot(
        hidden,
        down_rows,
        preferred_element_type=jnp.float32,
    )
    return (mixed_rows + reduced).astype(jnp.bfloat16)


def layer_kernel(
    x_ref,
    gain_ref,
    mlp_gain_ref,
    spots_ref,
    cols_ref,
    counts_ref,
    w_hbm,
    mix_hbm,
    up_hbm,
    down_hbm,
    out_ref,
    w_ref,
    mix_ref,
    up_all,
    down_all,
    normed,
    kv_out,
    memory,
    q_out,
    q_in,
    o_out,
    o_in,
    global_sum,
    global_kv,
    mixed,
    hidden,
    load_sem,
    kv_send,
    kv_recv,
    q_send,
    q_recv,
    o_send,
    o_recv,
    z_send,
    z_recv,
    swap_send,
    swap_recv,
):
    n = HEADS
    rows, width = x_ref.shape
    half = rows // 2
    blocks = rows // BLOCK
    slots = cols_ref.shape[0]
    count = spots_ref.shape[1]
    deep = n // 4
    me, g = lax.axis_index("seq"), lax.axis_index("groups")
    z, y, c = me // 4, me // 2 % 2, me % 2
    f32, bf16 = jnp.float32, jnp.bfloat16

    part = (up_hbm.shape[0] // 2, down_hbm.shape[0] // 2)

    def hop_views(piece):
        return [
            whole.at[piece, y, c, pl.ds(g * size, size)]
            for whole, size in zip((up_all, down_all), part)
        ]

    def load(source, target, at):
        return pltpu.make_async_copy(source, target, load_sem.at[at])

    loads = [
        load(up_hbm.at[pl.ds(g * part[0], part[0])], hop_views(z)[0], 0),
        load(down_hbm.at[pl.ds(g * part[1], part[1])], hop_views(z)[1], 1),
        load(w_hbm.at[:, pl.ds(width, 2 * width)], w_ref.at[:, pl.ds(width, 2 * width)], 2),
        load(w_hbm.at[:, pl.ds(0, width)], w_ref.at[:, pl.ds(0, width)], 3),
        load(mix_hbm, mix_ref, 4),
    ]
    for item in loads:
        item.start()

    barrier = pltpu.get_barrier_semaphore()

    def greet(step, carry):
        pl.semaphore_signal(
            barrier,
            inc=1,
            device_id={"seq": (me + step) % n},
            device_id_type=pl.DeviceIdType.MESH,
        )
        return carry

    lax.fori_loop(1, n, greet, 0)
    pl.semaphore_signal(
        barrier,
        inc=1,
        device_id={"groups": 1 - g, "seq": me},
        device_id_type=pl.DeviceIdType.MESH,
    )

    def remote(source, target, send, recv, where):
        return pltpu.make_async_remote_copy(
            src_ref=source,
            dst_ref=target,
            send_sem=send,
            recv_sem=recv,
            device_id=where,
            device_id_type=pl.DeviceIdType.MESH,
        )

    def kv_copy(owner, source):
        return remote(
            kv_out.at[owner],
            memory.at[pl.ds(source * blocks, blocks)],
            kv_send.at[owner],
            kv_recv.at[source],
            {"seq": owner},
        )

    def q_copy(owner, source):
        return remote(
            q_out.at[owner], q_in.at[source], q_send.at[owner], q_recv.at[source], {"seq": owner}
        )

    def o_copy(home, worker):
        return remote(
            o_out.at[home], o_in.at[worker], o_send.at[home], o_recv.at[worker], {"seq": home}
        )

    def hop_copies(way, hop, piece, to):
        return [
            remote(
                view,
                view,
                z_send.at[way, hop - 1, kind],
                z_recv.at[piece, kind],
                {"seq": to * 4 + y * 2 + c},
            )
            for kind, view in enumerate(hop_views(piece))
        ]

    def hop_sends(hop, act):
        for way, d in enumerate((1, -1)):
            piece, to = z - d * (hop - 1), z + d

            @pl.when((piece >= 0) & (piece < deep) & (to >= 0) & (to < deep))
            def _():
                for copy in hop_copies(way, hop, piece, to):
                    act(copy)

    def hop_waits(hop):
        for way, d in enumerate((1, -1)):
            piece = z - d * hop

            @pl.when((piece >= 0) & (piece < deep))
            def _():
                for copy in hop_copies(way, hop, piece, z):
                    copy.wait_recv()

    def y_copies(row):
        to = {"seq": me + 2 - 4 * y}
        return [
            remote(
                whole.at[:, row, c, pl.ds(g * size, size)],
                whole.at[:, row, c, pl.ds(g * size, size)],
                swap_send.at[0, kind],
                swap_recv.at[0, kind],
                to,
            )
            for kind, (whole, size) in enumerate(zip((up_all, down_all), part))
        ]

    def x_copies(turn, row, side):
        to = {"groups": 1 - g, "seq": me}
        return [
            remote(
                whole.at[:, row, c, pl.ds(side * size, size)],
                whole.at[:, row, c, pl.ds(side * size, size)],
                swap_send.at[1 + turn, kind],
                swap_recv.at[1 + turn, kind],
                to,
            )
            for kind, (whole, size) in enumerate(zip((up_all, down_all), part))
        ]

    def core_copies(core):
        to = {"seq": me + 1 - 2 * c}
        return [
            remote(
                whole.at[:, :, core],
                whole.at[:, :, core],
                swap_send.at[3, kind],
                swap_recv.at[3, kind],
                to,
            )
            for kind, whole in enumerate((up_all, down_all))
        ]

    def start(copies):
        for copy in copies:
            copy.start()

    def arrived(copies):
        for copy in copies:
            copy.wait_recv()

    def norm_rows(i, carry):
        at = pl.ds(pl.multiple_of(i * BLOCK, BLOCK), BLOCK)
        normed[at, :] = layer_norm(x_ref[at, :], gain_ref[...]).astype(bf16)
        return carry

    loads[0].wait()
    loads[1].wait()
    pl.semaphore_wait(barrier, n)
    hop_sends(1, lambda copy: copy.start())
    lax.fori_loop(0, blocks, norm_rows, 0)

    def quad_of(i):
        flip_high, flip_low = i // 2, i % 2
        return (z // 2 + flip_high) % 2 * 2 + (z % 2 + flip_low) % 2

    def member(quad, inner):
        return quad * 4 + (me + inner) % 4

    def project(first, quad):
        columns = pl.ds(pl.multiple_of(first * width + quad * 256, 256), 256)
        return jnp.dot(normed[...], w_ref[:, columns], preferred_element_type=f32)

    loads[2].wait()

    def kv_quad(i, carry):
        quad = quad_of(i)
        keys = project(1, quad)
        values = project(2, quad)
        for pair in range(2):
            at = slice(pair * 128, pair * 128 + 128)
            first, second = swap_halves(keys[:, at], values[:, at])
            kv_out[quad * 4 + 2 * pair] = first.astype(bf16).reshape(blocks, BLOCK, 128)
            kv_out[quad * 4 + 2 * pair + 1] = second.astype(bf16).reshape(blocks, BLOCK, 128)
        return carry

    def q_quad(i, carry):
        quad = quad_of(i)
        queries = project(0, quad) * 0.125
        for pair in range(2):
            both = queries[:, pair * 128 : pair * 128 + 128]
            first, second = swap_halves(both[:half], both[half:])
            head = quad * 4 + 2 * pair
            q_out[head] = first.astype(bf16)
            q_out[head + 1] = second.astype(bf16)
        return carry

    def send_each(first, last, copy):
        def send(i, carry):
            owner = member(quad_of(i // 4), i)

            @pl.when(owner != me)
            def _():
                copy(owner, me).start()

            return carry

        lax.fori_loop(first * 4, last * 4, send, 0)

    def kv_quad_sent(i, carry):
        kv_quad(i, carry)
        send_each(i, i + 1, kv_copy)
        return carry

    lax.fori_loop(0, 2, kv_quad_sent, 0)
    hop_waits(1)
    hop_sends(2, lambda copy: copy.start())
    lax.fori_loop(2, 4, kv_quad, 0)
    loads[3].wait()
    lax.fori_loop(0, 4, q_quad, 0)
    hop_waits(2)
    hop_sends(3, lambda copy: copy.start())
    send_each(2, 4, kv_copy)
    send_each(0, 2, q_copy)

    memory[pl.ds(me * blocks, blocks)] = kv_out[me]
    q_in[me] = q_out[me]

    global_sum[...] = jnp.zeros_like(global_sum)
    spots = spots_ref[...]
    spots_column = jnp.transpose(jnp.broadcast_to(spots.astype(f32), (128, count)))
    spots_column = spots_column[:, :1].astype(jnp.int32)

    def arrive(step, carry):
        source = member(quad_of(step // 4), step)

        @pl.when(source != me)
        def _():
            kv_copy(me, source).wait_recv()

        offset = spots_column - source * rows
        spot = lax.broadcasted_iota(jnp.int32, (count, rows), 1)
        chosen = jnp.where(spot == offset, 1.0, 0.0).astype(bf16)
        chunk = memory[pl.ds(source * blocks, blocks)].reshape(rows, 128)
        global_sum[...] += jnp.dot(chosen, chunk, preferred_element_type=f32)

        @pl.when(step == 4)
        def _():
            hop_waits(3)
            start(y_copies(y) + x_copies(0, y, g))

        @pl.when(step == 8)
        def _():
            def sent_far(i, carry):
                kv_copy(member(quad_of(i // 4), i), me).wait_send()
                return carry

            lax.fori_loop(8, n, sent_far, 0)
            send_each(2, 4, q_copy)

        return carry

    lax.fori_loop(0, n, arrive, 0)
    global_kv[...] = global_sum[...].astype(bf16)
    arrived(y_copies(1 - y))
    start(x_copies(1, 1 - y, g))
    spot_block = lax.shift_right_logical(spots, BLOCK.bit_length() - 1)

    def serve(step, carry):
        source = member(quad_of(step // 4 % 2 * 2 + step // 8), step)

        @pl.when(source != me)
        def _():
            q_copy(me, source).wait_recv()

        packed = q_in[source].astype(f32)
        low = lax.broadcasted_iota(jnp.int32, packed.shape, 1) < 64
        top = jnp.where(low, packed, 0.0).astype(bf16)
        bottom = jnp.where(low, pltpu.roll(packed, 64, 1), 0.0).astype(bf16)
        queries = jnp.concatenate((top, bottom), axis=0)
        results = []
        for r in range(blocks):
            block = source * blocks + r
            used = counts_ref[block]
            excluded = jnp.zeros((1, count), f32)
            parts = []
            for j in range(slots):
                listed = jnp.where(j < used, cols_ref[j, block], -1)
                excluded = jnp.where(spot_block == listed, MASKED, excluded)
                parts.append(jnp.full((1, BLOCK), jnp.where(j < used, 0.0, MASKED), f32))
            bias = jnp.concatenate(parts + [excluded], axis=1)
            picked = [memory[cols_ref[j, block]] for j in range(slots)]
            kv = jnp.concatenate(picked + [global_kv[...]], axis=0)
            scores = lax.dot_general(
                queries[r * BLOCK : (r + 1) * BLOCK],
                kv,
                (((1,), (1,)), ((), ())),
                preferred_element_type=f32,
            )
            weights = jnp.exp(scores + bias)
            totals = jnp.sum(weights, axis=1, keepdims=True)
            scale = jnp.where(totals > 1.0, 2.0**-10, 1.0)
            probs = (weights * (1.0 / (totals * scale))).astype(bf16)
            results.append(jnp.dot(probs, kv, preferred_element_type=f32) * scale)
        result = jnp.concatenate(results, axis=0)
        top, bottom = result[:half], result[half:]
        o_out[source] = jnp.where(low, pltpu.roll(top, 64, 1), bottom).astype(bf16)

        @pl.when(source != me)
        def _():
            o_copy(source, me).start()

        @pl.when(step == n - 4)
        def _():
            arrived(x_copies(0, y, 1 - g) + x_copies(1, 1 - y, 1 - g))
            start(core_copies(c))

        return carry

    lax.fori_loop(0, n, serve, 0)
    o_in[me] = o_out[me]

    def settle(step, carry):
        peer = (me + step) % n

        @pl.when((peer // 8 + me // 8) % 2 == 0)
        def _():
            kv_copy(peer, me).wait_send()

        q_copy(peer, me).wait_send()
        o_copy(me, peer).wait_recv()
        return carry

    lax.fori_loop(1, n, settle, 0)

    for pair in range(n // 2):
        first = o_in[2 * pair].astype(f32)
        second = o_in[2 * pair + 1].astype(f32)
        top, bottom = swap_halves(first, second)
        at = slice(pair * 128, pair * 128 + 128)
        normed[:half, at] = top.astype(bf16)
        normed[half:, at] = bottom.astype(bf16)

    loads[4].wait()

    def mix(i, carry):
        at = pl.ds(pl.multiple_of(i * 256, 256), 256)
        mixed[:, at] = x_ref[:, at].astype(f32) + jnp.dot(
            normed[...], mix_ref[:, at], preferred_element_type=f32
        )
        return carry

    lax.fori_loop(0, width // 256, mix, 0)

    def norm_again(i, carry):
        at = pl.ds(pl.multiple_of(i * BLOCK, BLOCK), BLOCK)
        normed[at, :] = layer_norm(mixed[at, :], mlp_gain_ref[...]).astype(bf16)
        return carry

    lax.fori_loop(0, blocks, norm_again, 0)
    arrived(core_copies(1 - c)[:1])

    def expand(i, carry):
        up = jnp.concatenate((up_all[i // 2, i % 2, 0], up_all[i // 2, i % 2, 1]), axis=1)
        units = jnp.dot(normed[...], up, preferred_element_type=f32)
        hidden[:, pl.ds(pl.multiple_of(i * 256, 256), 256)] = jax.nn.gelu(
            units, approximate=True
        ).astype(bf16)
        return carry

    lax.fori_loop(0, n // 2, expand, 0)

    arrived(core_copies(1 - c)[1:])

    def contract(i, carry):
        at = pl.ds(pl.multiple_of(i * 256, 256), 256)
        down = down_all[:, :, :, :, at].reshape(hidden.shape[1], 256)
        out_ref[:, at] = (
            mixed[:, at] + jnp.dot(hidden[...], down, preferred_element_type=f32)
        ).astype(bf16)
        return carry

    lax.fori_loop(0, width // 256, contract, 0)

    def finish(step, carry):
        o_copy((me + step) % n, me).wait_send()
        return carry

    lax.fori_loop(1, n, finish, 0)
    for hop in range(1, deep):
        hop_sends(hop, lambda copy: copy.wait_send())
    for copy in y_copies(y) + x_copies(0, y, g) + x_copies(1, 1 - y, g) + core_copies(c):
        copy.wait_send()


def whole_layer(
    features,
    attention_gain,
    qkv_weight,
    out_weight,
    mlp_gain,
    up_weight,
    down_weight,
    block_columns,
    block_counts,
    global_nodes,
):
    n = HEADS
    rows, width = features.shape
    half, blocks, deep = rows // 2, rows // BLOCK, n // 4
    count, unit = global_nodes.shape[0], up_weight.shape[1]
    keys = block_columns.shape[1] * BLOCK + count
    f32, bf16 = jnp.float32, jnp.bfloat16
    vmem = pl.BlockSpec(memory_space=pltpu.VMEM)
    smem = pl.BlockSpec(memory_space=pltpu.SMEM)
    hbm = pl.BlockSpec(memory_space=pl.ANY)
    flops = 2 * rows * width * (4 * width + 2 * n * unit) + 4 * rows * HEADS * 64 * keys
    dma = pltpu.SemaphoreType.DMA
    return pl.pallas_call(
        layer_kernel,
        out_shape=jax.ShapeDtypeStruct((rows, width), bf16),
        in_specs=[vmem] * 4 + [smem] * 2 + [hbm] * 4,
        out_specs=vmem,
        scratch_shapes=[
            pltpu.VMEM(qkv_weight.shape, bf16),
            pltpu.VMEM(out_weight.shape, bf16),
            pltpu.VMEM((deep, 2, 2, width, unit), bf16),
            pltpu.VMEM((deep, 2, 2, unit, width), bf16),
            pltpu.VMEM((rows, width), bf16),
            pltpu.VMEM((n, blocks, BLOCK, 128), bf16),
            pltpu.VMEM((n * blocks, BLOCK, 128), bf16),
            pltpu.VMEM((n, half, 128), bf16),
            pltpu.VMEM((n, half, 128), bf16),
            pltpu.VMEM((n, half, 128), bf16),
            pltpu.VMEM((n, half, 128), bf16),
            pltpu.VMEM((count, 128), f32),
            pltpu.VMEM((count, 128), bf16),
            pltpu.VMEM((rows, width), f32),
            pltpu.VMEM((rows, n * unit), bf16),
            dma((5,)),
        ]
        + [dma((n,))] * 6
        + [dma((2, deep - 1, 2)), dma((deep, 2)), dma((4, 2)), dma((4, 2))],
        compiler_params=pltpu.CompilerParams(
            collective_id=1, has_side_effects=True, vmem_limit_bytes=44 * 2**20
        ),
        cost_estimate=pl.CostEstimate(
            flops=flops, bytes_accessed=2**24, transcendentals=rows * HEADS * keys
        ),
        name="layer",
    )(
        features,
        attention_gain[None, :],
        mlp_gain[None, :],
        global_nodes[None, :],
        block_columns.T,
        block_counts,
        qkv_weight,
        out_weight,
        up_weight,
        down_weight,
    )


def solution(mesh):
    in_specs = (
        P(("groups", "seq"), None),
        P(),
        P(),
        P(),
        P(),
        P(None, "seq"),
        P("seq", None),
        P("groups", None),
        P("groups"),
        P("groups"),
    )
    out_specs = P(("groups", "seq"), None)
    step = whole_layer if mesh.shape["seq"] == HEADS and mesh.shape["groups"] == 2 else on_device
    return jax.shard_map(
        step, mesh=mesh, in_specs=in_specs, out_specs=out_specs, check_vma=False
    )
```
